256 devices in a mesh: seq: 4 (over x), blk: 64 (over z, y, core).
Axes of the slice: x: 4, y: 4, z: 8, core: 2. Of those that a mesh axis runs over, the one named last changes fastest.
Arguments:
- queries: bfloat16 [32768, 3072], P(('blk', 'seq')), may hold values from -140 to 140
- key_states: bfloat16 [32768, 3072], P(('blk', 'seq')), may hold values from -4.5 to 4.5
- value_states: bfloat16 [32768, 3072], P(('blk', 'seq')), may hold values from -6 to 6
- grad_out: bfloat16 [32768, 3072], P(('blk', 'seq')), may hold values from -6 to 6
- clip_table: int32 [21, 4], replicated, may hold values from 0 to 511, as said below
- windows: int32 [21, 3], replicated, may hold values from 0 to 1
Outputs:
- attended: bfloat16 [32768, 3072], P(('blk', 'seq'))
- grad_queries: bfloat16 [32768, 3072], P(('blk', 'seq'))
- grad_keys: bfloat16 [32768, 3072], P(('blk', 'seq'))
- grad_values: bfloat16 [32768, 3072], P(('blk', 'seq'))
The draws below stay inside these ranges and needn't reach their ends.
Inputs may be any that keep to these rules, and one draw needn't show every extreme that they name: `clip_table`: clips lie end to end from tile 0 and cover all 512 tiles; a clip's tiles run frame by frame, each frame row by row; heights and widths of tiles are 1 or 2.
All inputs are finite; a program needn't handle non-finite values.
Results may differ from the reference program's by a relative error of at most 0.012.
Values may be sent and summed in bfloat16 or wider, within the bound.
A program may use at most 128 MiB of HBM per device.

```python
import math
import jax
import jax.numpy as jnp
from jax import lax

HEADS = 24
HD = 128
TILE = 64
TOK_DEV = 128
WIDTH = 3072
BLK = 512
NT = 32768
HALO = 448
CLIPS = 21
N_SEQ = 4


def paired_states(key):
    shape_all = (NT, WIDTH)
    base_query = jnp.clip(jax.random.normal(jax.random.fold_in(key, 101), shape_all, jnp.float32), -4.5, 4.5)
    base_key = jnp.clip(jax.random.normal(jax.random.fold_in(key, 102), shape_all, jnp.float32), -4.5, 4.5)
    return (base_query, base_key)


def draw_queries(key, part):
    return paired_states(key)[0].astype(jnp.bfloat16)


def draw_key_states(key, part):
    return paired_states(key)[1].astype(jnp.bfloat16)


def draw_clip_table(key, part):
    per_block = BLK // TILE
    all_tiles = NT // TILE
    random_count = CLIPS - 6
    heights = jax.random.randint(jax.random.fold_in(key, 201), (random_count,), 1, 3)
    widths = jax.random.randint(jax.random.fold_in(key, 202), (random_count,), 1, 3)
    frames = jax.random.randint(jax.random.fold_in(key, 203), (random_count,), 1, per_block // 2 + 1)
    tile_counts = frames * heights * widths
    opening = 3 * per_block + 1
    starts = opening + jnp.cumsum(tile_counts) - tile_counts
    filler_start = opening + jnp.sum(tile_counts)
    fixed_rows = jnp.array([[0, per_block - 5, 1, 1], [per_block - 5, 3, 2, 2], [per_block + 7, 2 * per_block - 14, 1, 1], [3 * per_block - 7, 2, 2, 2]], dtype=jnp.int32)
    random_rows = jnp.stack((starts, frames, heights, widths), axis=1).astype(jnp.int32)
    filler_row = jnp.stack([filler_start, all_tiles - 1 - filler_start, jnp.int32(1), jnp.int32(1)]).astype(jnp.int32)[None, :]
    final_row = jnp.array([[all_tiles - 1, 1, 1, 1]], dtype=jnp.int32)
    return jnp.concatenate((fixed_rows, random_rows, filler_row, final_row), axis=0)


def draw_windows(key, part):
    values = jax.random.randint(jax.random.fold_in(key, 301), (CLIPS, 3), 0, 2)
    clip_index = jnp.arange(CLIPS, dtype=jnp.int32)
    forced = (clip_index == 1) | (clip_index == 3)
    return jnp.where(forced[:, None], 1, values).astype(jnp.int32)


def steps_of(rng, shape, split, smallest, high):
    gain, own = 1.0, jax.random.fold_in(rng, 6)
    for dim, parts in split:
        draws = jnp.exp(jax.random.uniform(jax.random.fold_in(own, dim), (parts,), jnp.float32, smallest / len(split), high / len(split)))
        gain = gain * jnp.repeat(draws, shape[dim] // parts).reshape([-1 if axis == dim else 1 for axis in range(len(shape))])
    return gain


def bell_draw(stream_key, shape, scale, reach, cuts=(), kind=jnp.bfloat16):
    loudness = steps_of(stream_key, shape, cuts, -0.22, 0.18) if cuts else 1.0
    values = jax.random.normal(stream_key, shape, jnp.float32) * scale * loudness
    return jnp.minimum(jnp.maximum(values, -reach), reach).astype(kind)


def setup_inputs(seed: int = 0) -> dict:
    key_of = jax.random.split(jax.random.key(seed), 7)
    queries = draw_queries(jax.random.fold_in(key_of[6], 71), 0)
    key_states = draw_key_states(jax.random.fold_in(key_of[6], 71), 0)
    value_states = bell_draw(key_of[2], (NT, WIDTH), 1.0, 6.0, ((0, 256),))
    grad_out = bell_draw(key_of[3], (NT, WIDTH), 1.0, 6.0, ((0, 256),))
    clip_table = draw_clip_table(jax.random.fold_in(key_of[6], 71), 0)
    windows = draw_windows(jax.random.fold_in(key_of[6], 71), 0)
    return {"queries": queries, "key_states": key_states, "value_states": value_states, "grad_out": grad_out, "clip_table": clip_table, "windows": windows}


def coords(positions, clip_table, windows, total):
    tile_index = positions // TILE
    number = clip_table.shape[0]
    clip_owner = lax.optimization_barrier(jnp.sum((clip_table[None, :, 0] <= tile_index[:, None]).astype(jnp.int32), axis=1)) - 1
    inside_grid = (positions >= 0) & (positions < total)
    selector = (jnp.arange(number, dtype=jnp.int32)[None, :] == clip_owner[:, None]).astype(jnp.int32)
    first_tile = lax.optimization_barrier(jnp.sum(selector * clip_table[None, :, 0], axis=1))
    tile_rows = jnp.maximum(lax.optimization_barrier(jnp.sum(selector * clip_table[None, :, 2], axis=1)), 1)
    tile_cols = jnp.maximum(lax.optimization_barrier(jnp.sum(selector * clip_table[None, :, 3], axis=1)), 1)
    reach_frame = lax.optimization_barrier(jnp.sum(selector * windows[None, :, 0], axis=1))
    reach_row = lax.optimization_barrier(jnp.sum(selector * windows[None, :, 1], axis=1))
    reach_col = lax.optimization_barrier(jnp.sum(selector * windows[None, :, 2], axis=1))
    local_tile = tile_index - first_tile
    frame_of = local_tile // (tile_rows * tile_cols)
    row_of = local_tile // tile_cols % tile_rows
    col_of = local_tile % tile_cols
    clip_owner = jnp.where(inside_grid, clip_owner, -1)
    return (clip_owner, frame_of, row_of, col_of, reach_frame, reach_row, reach_col, inside_grid)

def allowed_pairs(query_geo, key_geo):
    q_owner, q_frame, q_row, q_col, reach_frame, reach_row, reach_col, q_inside = query_geo
    k_owner, k_frame, k_row, k_col, unused_frame, unused_row, unused_col, k_inside = key_geo
    same_clip = (q_owner[:, None] == k_owner[None, :]) & q_inside[:, None] & k_inside[None, :]
    near_frame = jnp.abs(q_frame[:, None] - k_frame[None, :]) <= reach_frame[:, None]
    near_row = jnp.abs(q_row[:, None] - k_row[None, :]) <= reach_row[:, None]
    near_col = jnp.abs(q_col[:, None] - k_col[None, :]) <= reach_col[:, None]
    return same_clip & near_frame & near_row & near_col

def split_heads(array):
    return array.reshape(array.shape[0], HEADS, HD).astype(jnp.float32)

def reference(queries, key_states, value_states, grad_out, clip_table, windows):
    total = queries.shape[0]
    block = N_SEQ * TOK_DEV
    span = block + 2 * HALO
    count_blocks = total // block
    scale = 1.0 / math.sqrt(HD)
    padding = ((HALO, HALO), (0, 0))
    padded_q = jnp.pad(queries, padding)
    padded_k = jnp.pad(key_states, padding)
    padded_v = jnp.pad(value_states, padding)
    padded_g = jnp.pad(grad_out, padding)

    def forward_block(index):
        anchor = (index * block).astype(jnp.int32)
        own_pos = anchor + jnp.arange(block, dtype=jnp.int32)
        ext_pos = anchor - HALO + jnp.arange(span, dtype=jnp.int32)
        mask = allowed_pairs(coords(own_pos, clip_table, windows, total), coords(ext_pos, clip_table, windows, total))
        q_part = split_heads(lax.dynamic_slice_in_dim(queries, anchor, block, 0))
        g_part = split_heads(lax.dynamic_slice_in_dim(grad_out, anchor, block, 0))
        k_ext = split_heads(lax.dynamic_slice_in_dim(padded_k, anchor, span, 0))
        v_ext = split_heads(lax.dynamic_slice_in_dim(padded_v, anchor, span, 0))
        scores = jnp.einsum('qhd,khd->hqk', q_part, k_ext) * scale
        row_max = lax.optimization_barrier(jnp.max(jnp.where(mask[None], scores, -jnp.inf), axis=2))
        weights = jnp.where(mask[None], jnp.exp(scores - row_max[:, :, None]), 0.0)
        row_total = lax.optimization_barrier(jnp.sum(weights, axis=2))
        probs = weights / row_total[:, :, None]
        probs_low = probs.astype(jnp.bfloat16)
        attended = jnp.einsum('hqk,khd->qhd', probs_low.astype(jnp.float32), v_ext).astype(jnp.bfloat16)
        delta = lax.optimization_barrier(jnp.sum(g_part * attended.astype(jnp.float32), axis=2))
        dprobs = jnp.einsum('qhd,khd->hqk', g_part, v_ext)
        dscores = (probs * (dprobs - delta.T[:, :, None]) * scale).astype(jnp.bfloat16)
        grad_q = jnp.einsum('hqk,khd->qhd', dscores.astype(jnp.float32), k_ext).astype(jnp.bfloat16)
        return (attended.reshape(block, HEADS * HD), grad_q.reshape(block, HEADS * HD), row_max.T, row_total.T, delta)
    blocks = jnp.arange(count_blocks, dtype=jnp.int32)
    attended, grad_q, row_max, row_total, delta = lax.map(forward_block, blocks)
    attended = attended.reshape(total, HEADS * HD)
    grad_q = grad_q.reshape(total, HEADS * HD)
    pad_stats = ((HALO, HALO), (0, 0))
    max_pad = jnp.pad(row_max.reshape(total, HEADS), pad_stats)
    total_pad = jnp.pad(row_total.reshape(total, HEADS), pad_stats, constant_values=1.0)
    delta_pad = jnp.pad(delta.reshape(total, HEADS), pad_stats)

    def backward_block(index):
        anchor = (index * block).astype(jnp.int32)
        own_pos = anchor + jnp.arange(block, dtype=jnp.int32)
        ext_pos = anchor - HALO + jnp.arange(span, dtype=jnp.int32)
        mask = allowed_pairs(coords(ext_pos, clip_table, windows, total), coords(own_pos, clip_table, windows, total))
        k_own = split_heads(lax.dynamic_slice_in_dim(key_states, anchor, block, 0))
        v_own = split_heads(lax.dynamic_slice_in_dim(value_states, anchor, block, 0))
        q_ext = split_heads(lax.dynamic_slice_in_dim(padded_q, anchor, span, 0))
        g_ext = split_heads(lax.dynamic_slice_in_dim(padded_g, anchor, span, 0))
        max_ext = lax.dynamic_slice_in_dim(max_pad, anchor, span, 0)
        total_ext = lax.dynamic_slice_in_dim(total_pad, anchor, span, 0)
        delta_ext = lax.dynamic_slice_in_dim(delta_pad, anchor, span, 0)
        scores = jnp.einsum('qhd,khd->hqk', q_ext, k_own) * scale
        weights = jnp.where(mask[None], jnp.exp(scores - max_ext.T[:, :, None]), 0.0)
        probs = weights / total_ext.T[:, :, None]
        probs_low = probs.astype(jnp.bfloat16)
        grad_v = jnp.einsum('hqk,qhd->khd', probs_low.astype(jnp.float32), g_ext).astype(jnp.bfloat16)
        dprobs = jnp.einsum('qhd,khd->hqk', g_ext, v_own)
        dscores = (probs * (dprobs - delta_ext.T[:, :, None]) * scale).astype(jnp.bfloat16)
        grad_k = jnp.einsum('hqk,qhd->khd', dscores.astype(jnp.float32), q_ext).astype(jnp.bfloat16)
        return (grad_k.reshape(block, HEADS * HD), grad_v.reshape(block, HEADS * HD))
    grad_k, grad_v = lax.map(backward_block, blocks)
    return (attended, grad_q, grad_k.reshape(total, HEADS * HD), grad_v.reshape(total, HEADS * HD))
```

```python
import functools
import math

import jax
import jax.numpy as jnp
from jax import lax
from jax.experimental import pallas as pl
from jax.experimental.pallas import tpu as pltpu
from jax.sharding import PartitionSpec as P

HD = 128
TILE = 64
HALO = 448
MASKED = -1e30
MESH = pl.DeviceIdType.MESH


def nt(left, right):
    return lax.dot_general(
        left, right, (((1,), (1,)), ((), ())), preferred_element_type=jnp.float32
    )


def nn(left, right):
    return jnp.dot(left, right, preferred_element_type=jnp.float32)


def tn(left, right):
    return lax.dot_general(
        left, right, (((0,), (0,)), ((), ())), preferred_element_type=jnp.float32
    )


def fill_bias(bias, clip_table, windows, first_tile, total_tiles):
    shape = bias.shape
    q_tile = first_tile + lax.broadcasted_iota(jnp.int32, shape, 0)
    k_tile = first_tile - HALO // TILE + (lax.broadcasted_iota(jnp.int32, shape, 1) >> 6)
    none = jnp.full(shape, -1, jnp.int32)
    zero = jnp.zeros(shape, jnp.int32)
    one = jnp.ones(shape, jnp.int32)
    q_clip, k_clip, start = none, none, zero
    rows, cols = one, one
    reach_f, reach_r, reach_c = zero, zero, zero
    for clip in range(clip_table.shape[0]):
        begin = clip_table[clip, 0]
        here = q_tile >= begin
        q_clip = jnp.where(here, clip, q_clip)
        k_clip = jnp.where(k_tile >= begin, clip, k_clip)
        start = jnp.where(here, begin, start)
        rows = jnp.where(here, clip_table[clip, 2], rows)
        cols = jnp.where(here, clip_table[clip, 3], cols)
        reach_f = jnp.where(here, windows[clip, 0], reach_f)
        reach_r = jnp.where(here, windows[clip, 1], reach_r)
        reach_c = jnp.where(here, windows[clip, 2], reach_c)

    def place(tile):
        local = tile - start
        line = jnp.where(cols == 2, local >> 1, local)
        frame = jnp.where(rows == 2, line >> 1, line)
        return frame, line - frame * rows, local - line * cols

    q_frame, q_row, q_col = place(q_tile)
    k_frame, k_row, k_col = place(k_tile)
    allowed = (
        (q_clip == k_clip)
        & (k_tile >= 0)
        & (k_tile < total_tiles)
        & (jnp.abs(q_frame - k_frame) <= reach_f)
        & (jnp.abs(q_row - k_row) <= reach_r)
        & (jnp.abs(q_col - k_col) <= reach_c)
    )
    bias[...] = jnp.where(allowed, 0.0, MASKED).astype(jnp.float32)


def kernel(
    seq_axis,
    blk_axis,
    n_seq,
    n_blk,
    heads,
    q_in,
    k_in,
    v_in,
    g_in,
    clip_table,
    windows,
    att_out,
    dq_out,
    dk_out,
    dv_out,
    kv,
    qg,
    relay_in,
    results,
    relay_out,
    acc,
    rim_send,
    rim_recv,
    bias,
    in_recv,
    in_send,
    hop_recv,
    pass_send,
    halo_recv,
    halo_send,
    rim_recv_sem,
    rim_send_sem,
    out_recv,
    out_send,
    back_recv,
    back_send,
):
    scale = 1.0 / math.sqrt(HD)
    tok = q_in.shape[0]
    block = tok * n_seq
    me = lax.axis_index(seq_axis)
    blk = lax.axis_index(blk_axis)
    right = lax.rem(me + 1, n_seq)
    left = lax.rem(me + n_seq - 1, n_seq)
    far = lax.rem(me + 2, n_seq)
    above = lax.rem(blk + 1, n_blk)
    below = lax.rem(blk + n_blk - 1, n_blk)
    to_right, to_left = {seq_axis: right}, {seq_axis: left}
    to_above, to_below = {blk_axis: above}, {blk_axis: below}

    sources = (k_in, v_in, q_in, g_in)
    outs = (att_out, dq_out, dk_out, dv_out)

    def landing(array, stage, origin):
        row = origin * tok
        if array < 2:
            return kv.at[array, stage, pl.ds(HALO + row, tok), :]
        return qg.at[array - 2, stage, pl.ds(row, tok), :]

    def columns(ref, owner, stage):
        start = pl.multiple_of((owner * heads + stage) * HD, HD)
        return ref.at[:, pl.ds(start, HD)]

    def send(src, dst, send_sem, recv_sem, device):
        pltpu.make_async_remote_copy(
            src_ref=src,
            dst_ref=dst,
            send_sem=send_sem,
            recv_sem=recv_sem,
            device_id=device,
            device_id_type=MESH,
        ).start()

    def wait(ref, sem):
        pltpu.make_async_copy(ref, ref, sem).wait()

    def issue_in(stage):
        for array, src in enumerate(sources):
            via = to_right if array % 2 == 0 else to_left
            arrived = in_recv.at[stage, array]
            sent = in_send.at[array]
            send(
                columns(src, far, stage),
                relay_in.at[array, stage],
                sent,
                hop_recv.at[stage, array],
                via,
            )
            send(columns(src, right, stage), landing(array, stage, me), sent, arrived, to_right)
            send(columns(src, left, stage), landing(array, stage, me), sent, arrived, to_left)
            pltpu.make_async_copy(
                columns(src, me, stage), landing(array, stage, me), arrived
            ).start()

    def pass_in(stage):
        for array in range(4):
            wait(relay_in.at[array, stage], hop_recv.at[stage, array])
            onward, origin = (to_right, left) if array % 2 == 0 else (to_left, right)
            send(
                relay_in.at[array, stage],
                landing(array, stage, origin),
                pass_send.at[array],
                in_recv.at[stage, array],
                onward,
            )

    def send_halo(stage):
        for array in range(2):
            wait(kv.at[array, stage, pl.ds(HALO, block), :], in_recv.at[stage, array])
            sent = halo_send.at[array]
            send(
                kv.at[array, stage, pl.ds(block, HALO), :],
                kv.at[array, stage, pl.ds(0, HALO), :],
                sent,
                halo_recv.at[stage, array, 0],
                to_above,
            )
            send(
                kv.at[array, stage, pl.ds(HALO, HALO), :],
                kv.at[array, stage, pl.ds(HALO + block, HALO), :],
                sent,
                halo_recv.at[stage, array, 1],
                to_below,
            )

    def compute(stage):
        for array in range(2):
            wait(qg.at[array, stage], in_recv.at[stage, 2 + array])
            wait(kv.at[array, stage, pl.ds(0, HALO), :], halo_recv.at[stage, array, 0])
            wait(kv.at[array, stage, pl.ds(HALO + block, HALO), :], halo_recv.at[stage, array, 1])
        rows = block // 2
        span = rows + 2 * HALO
        for part in range(2):
            low = part * rows
            q = qg[0, stage, low : low + rows, :]
            g = qg[1, stage, low : low + rows, :]
            k = kv[0, stage, low : low + span, :]
            v = kv[1, stage, low : low + span, :]
            product = nt(q, k)
            per_part = rows // TILE
            scores = jnp.concatenate(
                [
                    product[t * TILE : (t + 1) * TILE] * scale
                    + bias[part * per_part + t : part * per_part + t + 1, low : low + span]
                    for t in range(per_part)
                ],
                axis=0,
            )
            row_max = jnp.max(scores, axis=1, keepdims=True)
            weights = jnp.exp(scores - row_max)
            total = jnp.sum(weights, axis=1, keepdims=True)
            probs = weights * (1.0 / total)
            probs_low = probs.astype(jnp.bfloat16)
            attended = nn(probs_low, v).astype(jnp.bfloat16)
            delta = jnp.sum(
                g.astype(jnp.float32) * attended.astype(jnp.float32), axis=1, keepdims=True
            )
            dscores = (probs * (nt(g, v) - delta) * scale).astype(jnp.bfloat16)
            results[0, stage, low : low + rows, :] = attended
            results[1, stage, low : low + rows, :] = nn(dscores, k).astype(jnp.bfloat16)
            for index, grad in enumerate((tn(dscores, q), tn(probs_low, g))):
                if part == 0:
                    acc[index, stage, 0:span, :] = grad
                else:
                    shared = span - rows
                    acc[index, stage, rows:span, :] += grad[:shared]
                    acc[index, stage, span : span + rows, :] = grad[shared:]
        for index in range(2):
            rim_send[index, stage, 0] = acc[index, stage, 0:HALO, :].astype(jnp.bfloat16)
            rim_send[index, stage, 1] = acc[
                index, stage, HALO + block : 2 * HALO + block, :
            ].astype(jnp.bfloat16)
            sent = rim_send_sem.at[index]
            send(
                rim_send.at[index, stage, 0],
                rim_recv.at[index, stage, 1],
                sent,
                rim_recv_sem.at[stage, index, 1],
                to_below,
            )
            send(
                rim_send.at[index, stage, 1],
                rim_recv.at[index, stage, 0],
                sent,
                rim_recv_sem.at[stage, index, 0],
                to_above,
            )

    def finish(stage):
        for index in range(2):
            wait(rim_recv.at[index, stage, 0], rim_recv_sem.at[stage, index, 0])
            wait(rim_recv.at[index, stage, 1], rim_recv_sem.at[stage, index, 1])
            edge = block - HALO
            acc[index, stage, HALO : 2 * HALO, :] += rim_recv[index, stage, 0].astype(jnp.float32)
            acc[index, stage, HALO + edge : HALO + block, :] += rim_recv[index, stage, 1].astype(
                jnp.float32
            )
            results[2 + index, stage] = acc[index, stage, HALO : HALO + block, :].astype(
                jnp.bfloat16
            )

    def rows_of(array, stage, owner):
        return results.at[array, stage, pl.ds(pl.multiple_of(owner * tok, tok), tok), :]

    def issue_out(stage, arrays):
        for array in arrays:
            via = to_right if array % 2 == 0 else to_left
            arrived = out_recv.at[array]
            sent = out_send.at[array]
            mine = columns(outs[array], me, stage)
            send(
                rows_of(array, stage, far),
                relay_out.at[array, stage],
                sent,
                back_recv.at[stage, array],
                via,
            )
            send(rows_of(array, stage, right), mine, sent, arrived, to_right)
            send(rows_of(array, stage, left), mine, sent, arrived, to_left)
            pltpu.make_async_copy(rows_of(array, stage, me), mine, arrived).start()

    def pass_out(stage, arrays):
        for array in arrays:
            wait(relay_out.at[array, stage], back_recv.at[stage, array])
            onward, origin = (to_right, left) if array % 2 == 0 else (to_left, right)
            send(
                relay_out.at[array, stage],
                columns(outs[array], origin, stage),
                back_send.at[array],
                out_recv.at[array],
                onward,
            )

    barrier = pltpu.get_barrier_semaphore()
    for device in (to_right, to_left, to_above, to_below):
        pl.semaphore_signal(barrier, inc=1, device_id=device, device_id_type=MESH)
    pl.semaphore_wait(barrier, 4)

    issue_in(0)
    issue_in(1)
    tiles = block // TILE
    fill_bias(bias, clip_table, windows, blk * tiles, n_blk * tiles)

    def step(index, carry):
        def run(lag, action):
            stage = index - lag

            @pl.when((stage >= 0) & (stage < heads))
            def _():
                action(stage)

        run(0, pass_in)
        run(-2, lambda stage: pl.when(stage >= 2)(lambda: issue_in(stage)))
        run(0, send_halo)
        run(1, compute)
        run(2, finish)
        run(2, lambda stage: issue_out(stage, range(4)))
        run(3, lambda stage: pass_out(stage, range(4)))
        return carry

    lax.fori_loop(0, heads + 3, step, 0)

    for array in range(4):
        wait(outs[array], out_recv.at[array])
        wait(sources[array].at[:, pl.ds(0, 3 * heads * HD)], in_send.at[array])
        wait(relay_in.at[array], pass_send.at[array])
        wait(results.at[array, :, pl.ds(0, 3 * tok), :], out_send.at[array])
        wait(relay_out.at[array], back_send.at[array])
    for index in range(2):
        wait(rim_send.at[index], halo_send.at[index])
        wait(rim_send.at[index], rim_send_sem.at[index])


def on_device(n_seq, n_blk, queries, key_states, value_states, grad_out, clip_table, windows):
    tok, width = queries.shape
    heads = width // HD // n_seq
    block = tok * n_seq
    extended = block + 2 * HALO
    low = jnp.bfloat16
    hbm = pl.BlockSpec(memory_space=pl.ANY)
    smem = pl.BlockSpec(memory_space=pltpu.SMEM)
    dma = pltpu.SemaphoreType.DMA
    return pl.pallas_call(
        functools.partial(kernel, "seq", "blk", n_seq, n_blk, heads),
        out_shape=[jax.ShapeDtypeStruct((tok, width), low)] * 4,
        in_specs=[hbm] * 4 + [smem] * 2,
        out_specs=[hbm] * 4,
        scratch_shapes=[
            pltpu.VMEM((2, heads, extended, HD), low),
            pltpu.VMEM((2, heads, block, HD), low),
            pltpu.VMEM((4, heads, tok, HD), low),
            pltpu.VMEM((4, heads, block, HD), low),
            pltpu.VMEM((4, heads, tok, HD), low),
            pltpu.VMEM((2, heads, extended, HD), jnp.float32),
            pltpu.VMEM((2, heads, 2, HALO, HD), low),
            pltpu.VMEM((2, heads, 2, HALO, HD), low),
            pltpu.VMEM((block // TILE, extended), jnp.float32),
            dma((heads, 4)),
            dma((4,)),
            dma((heads, 4)),
            dma((4,)),
            dma((heads, 2, 2)),
            dma((2,)),
            dma((heads, 2, 2)),
            dma((2,)),
            dma((4,)),
            dma((4,)),
            dma((heads, 4)),
            dma((4,)),
        ],
        compiler_params=pltpu.CompilerParams(
            collective_id=0, has_side_effects=True, vmem_limit_bytes=60 * 1024 * 1024
        ),
        name="attention_with_exchange",
    )(queries, key_states, value_states, grad_out, clip_table, windows)


def solution(mesh):
    rows = P(("blk", "seq"), None)
    return jax.shard_map(
        functools.partial(on_device, mesh.shape["seq"], mesh.shape["blk"]),
        mesh=mesh,
        in_specs=(rows, rows, rows, rows, P(), P()),
        out_specs=(rows, rows, rows, rows),
        check_vma=False,
    )
```

```python
import functools
import math

import jax
import jax.numpy as jnp
from jax import lax
from jax.experimental import pallas as pl
from jax.experimental.pallas import tpu as pltpu
from jax.sharding import PartitionSpec as P

HD = 128
TILE = 64
HALO = 448
MASKED = -1e30
MESH = pl.DeviceIdType.MESH


def nt(left, right):
    return lax.dot_general(
        left, right, (((1,), (1,)), ((), ())), preferred_element_type=jnp.float32
    )


def nn(left, right):
    return jnp.dot(left, right, preferred_element_type=jnp.float32)


def tn(left, right):
    return lax.dot_general(
        left, right, (((0,), (0,)), ((), ())), preferred_element_type=jnp.float32
    )


def fill_bias(bias, clip_table, windows, first_tile, total_tiles):
    shape = bias.shape
    q_tile = first_tile + lax.broadcasted_iota(jnp.int32, shape, 0)
    k_tile = first_tile - HALO // TILE + (lax.broadcasted_iota(jnp.int32, shape, 1) >> 6)
    none = jnp.full(shape, -1, jnp.int32)
    zero = jnp.zeros(shape, jnp.int32)
    one = jnp.ones(shape, jnp.int32)
    q_clip, k_clip, start = none, none, zero
    rows, cols = one, one
    reach_f, reach_r, reach_c = zero, zero, zero
    for clip in range(clip_table.shape[0]):
        begin = clip_table[clip, 0]
        here = q_tile >= begin
        q_clip = jnp.where(here, clip, q_clip)
        k_clip = jnp.where(k_tile >= begin, clip, k_clip)
        start = jnp.where(here, begin, start)
        rows = jnp.where(here, clip_table[clip, 2], rows)
        cols = jnp.where(here, clip_table[clip, 3], cols)
        reach_f = jnp.where(here, windows[clip, 0], reach_f)
        reach_r = jnp.where(here, windows[clip, 1], reach_r)
        reach_c = jnp.where(here, windows[clip, 2], reach_c)

    def place(tile):
        local = tile - start
        line = jnp.where(cols == 2, local >> 1, local)
        frame = jnp.where(rows == 2, line >> 1, line)
        return frame, line - frame * rows, local - line * cols

    q_frame, q_row, q_col = place(q_tile)
    k_frame, k_row, k_col = place(k_tile)
    allowed = (
        (q_clip == k_clip)
        & (k_tile >= 0)
        & (k_tile < total_tiles)
        & (jnp.abs(q_frame - k_frame) <= reach_f)
        & (jnp.abs(q_row - k_row) <= reach_r)
        & (jnp.abs(q_col - k_col) <= reach_c)
    )
    bias[...] = jnp.where(allowed, 0.0, MASKED).astype(jnp.float32)


def kernel(
    seq_axis,
    blk_axis,
    n_seq,
    n_blk,
    heads,
    q_in,
    k_in,
    v_in,
    g_in,
    clip_table,
    windows,
    att_out,
    dq_out,
    dk_out,
    dv_out,
    kv,
    qg,
    relay_in,
    results,
    relay_out,
    acc,
    rim_send,
    rim_recv,
    bias,
    in_recv,
    in_send,
    hop_recv,
    pass_send,
    halo_recv,
    halo_send,
    rim_recv_sem,
    rim_send_sem,
    out_recv,
    out_send,
    back_recv,
    back_send,
):
    scale = 1.0 / math.sqrt(HD)
    tok = q_in.shape[0]
    block = tok * n_seq
    me = lax.axis_index(seq_axis)
    blk = lax.axis_index(blk_axis)
    right = lax.rem(me + 1, n_seq)
    left = lax.rem(me + n_seq - 1, n_seq)
    far = lax.rem(me + 2, n_seq)
    above = lax.rem(blk + 1, n_blk)
    below = lax.rem(blk + n_blk - 1, n_blk)
    to_right, to_left = {seq_axis: right}, {seq_axis: left}
    to_above, to_below = {blk_axis: above}, {blk_axis: below}

    sources = (k_in, v_in, q_in, g_in)
    outs = (att_out, dq_out, dk_out, dv_out)

    def landing(array, stage, origin):
        row = origin * tok
        if array < 2:
            return kv.at[array, stage, pl.ds(HALO + row, tok), :]
        return qg.at[array - 2, stage, pl.ds(row, tok), :]

    def columns(ref, owner, stage):
        start = pl.multiple_of((owner * heads + stage) * HD, HD)
        return ref.at[:, pl.ds(start, HD)]

    def send(src, dst, send_sem, recv_sem, device):
        pltpu.make_async_remote_copy(
            src_ref=src,
            dst_ref=dst,
            send_sem=send_sem,
            recv_sem=recv_sem,
            device_id=device,
            device_id_type=MESH,
        ).start()

    def wait(ref, sem):
        pltpu.make_async_copy(ref, ref, sem).wait()

    def issue_in(stage):
        for array, src in enumerate(sources):
            via = to_right if array % 2 == 0 else to_left
            send(
                columns(src, far, stage),
                relay_in.at[array, stage],
                in_send.at[array],
                hop_recv.at[stage, array],
                via,
            )
        for array, src in enumerate(sources):
            arrived = in_recv.at[stage, array]
            sent = in_send.at[array]
            send(columns(src, right, stage), landing(array, stage, me), sent, arrived, to_right)
            send(columns(src, left, stage), landing(array, stage, me), sent, arrived, to_left)
            pltpu.make_async_copy(
                columns(src, me, stage), landing(array, stage, me), arrived
            ).start()

    def pass_in(stage):
        for array in range(4):
            wait(relay_in.at[array, stage], hop_recv.at[stage, array])
            onward, origin = (to_right, left) if array % 2 == 0 else (to_left, right)
            send(
                relay_in.at[array, stage],
                landing(array, stage, origin),
                pass_send.at[array],
                in_recv.at[stage, array],
                onward,
            )

    def send_halo(stage):
        for array in range(2):
            wait(kv.at[array, stage, pl.ds(HALO, block), :], in_recv.at[stage, array])
            sent = halo_send.at[array]
            send(
                kv.at[array, stage, pl.ds(block, HALO), :],
                kv.at[array, stage, pl.ds(0, HALO), :],
                sent,
                halo_recv.at[stage, array, 0],
                to_above,
            )
            send(
                kv.at[array, stage, pl.ds(HALO, HALO), :],
                kv.at[array, stage, pl.ds(HALO + block, HALO), :],
                sent,
                halo_recv.at[stage, array, 1],
                to_below,
            )

    def compute(stage):
        for array in range(2):
            wait(qg.at[array, stage], in_recv.at[stage, 2 + array])
            wait(kv.at[array, stage, pl.ds(0, HALO), :], halo_recv.at[stage, array, 0])
            wait(kv.at[array, stage, pl.ds(HALO + block, HALO), :], halo_recv.at[stage, array, 1])
        rows = block // 2
        span = rows + 2 * HALO
        for part in range(2):
            low = part * rows
            q = qg[0, stage, low : low + rows, :]
            g = qg[1, stage, low : low + rows, :]
            k = kv[0, stage, low : low + span, :]
            v = kv[1, stage, low : low + span, :]
            product = nt(q, k)
            per_part = rows // TILE
            scores = jnp.concatenate(
                [
                    product[t * TILE : (t + 1) * TILE] * scale
                    + bias[part * per_part + t : part * per_part + t + 1, low : low + span]
                    for t in range(per_part)
                ],
                axis=0,
            )
            row_max = jnp.max(scores, axis=1, keepdims=True)
            weights = jnp.exp(scores - row_max)
            total = jnp.sum(weights, axis=1, keepdims=True)
            probs = weights * (1.0 / total)
            probs_low = probs.astype(jnp.bfloat16)
            attended = nn(probs_low, v).astype(jnp.bfloat16)
            delta = jnp.sum(
                g.astype(jnp.float32) * attended.astype(jnp.float32), axis=1, keepdims=True
            )
            dscores = (probs * (nt(g, v) - delta) * scale).astype(jnp.bfloat16)
            results[0, stage, low : low + rows, :] = attended
            results[1, stage, low : low + rows, :] = nn(dscores, k).astype(jnp.bfloat16)
            for index, grad in enumerate((tn(dscores, q), tn(probs_low, g))):
                if part == 0:
                    acc[index, stage, 0:span, :] = grad
                else:
                    shared = span - rows
                    acc[index, stage, rows:span, :] += grad[:shared]
                    acc[index, stage, span : span + rows, :] = grad[shared:]
        for index in range(2):
            rim_send[index, stage, 0] = acc[index, stage, 0:HALO, :].astype(jnp.bfloat16)
            rim_send[index, stage, 1] = acc[
                index, stage, HALO + block : 2 * HALO + block, :
            ].astype(jnp.bfloat16)
            sent = rim_send_sem.at[index]
            send(
                rim_send.at[index, stage, 0],
                rim_recv.at[index, stage, 1],
                sent,
                rim_recv_sem.at[stage, index, 1],
                to_below,
            )
            send(
                rim_send.at[index, stage, 1],
                rim_recv.at[index, stage, 0],
                sent,
                rim_recv_sem.at[stage, index, 0],
                to_above,
            )

    def finish(stage):
        for index in range(2):
            wait(rim_recv.at[index, stage, 0], rim_recv_sem.at[stage, index, 0])
            wait(rim_recv.at[index, stage, 1], rim_recv_sem.at[stage, index, 1])
            edge = block - HALO
            acc[index, stage, HALO : 2 * HALO, :] += rim_recv[index, stage, 0].astype(jnp.float32)
            acc[index, stage, HALO + edge : HALO + block, :] += rim_recv[index, stage, 1].astype(
                jnp.float32
            )
            results[2 + index, stage] = acc[index, stage, HALO : HALO + block, :].astype(
                jnp.bfloat16
            )

    def rows_of(array, stage, owner):
        return results.at[array, stage, pl.ds(pl.multiple_of(owner * tok, tok), tok), :]

    def issue_out(stage, arrays):
        for array in arrays:
            via = to_right if array % 2 == 0 else to_left
            send(
                rows_of(array, stage, far),
                relay_out.at[array, stage],
                out_send.at[array],
                back_recv.at[stage, array],
                via,
            )
        for array in arrays:
            arrived = out_recv.at[array]
            sent = out_send.at[array]
            mine = columns(outs[array], me, stage)
            send(rows_of(array, stage, right), mine, sent, arrived, to_right)
            send(rows_of(array, stage, left), mine, sent, arrived, to_left)
            pltpu.make_async_copy(rows_of(array, stage, me), mine, arrived).start()

    def pass_out(stage, arrays):
        for array in arrays:
            wait(relay_out.at[array, stage], back_recv.at[stage, array])
            onward, origin = (to_right, left) if array % 2 == 0 else (to_left, right)
            send(
                relay_out.at[array, stage],
                columns(outs[array], origin, stage),
                back_send.at[array],
                out_recv.at[array],
                onward,
            )

    barrier = pltpu.get_barrier_semaphore()
    for device in (to_right, to_left, to_above, to_below):
        pl.semaphore_signal(barrier, inc=1, device_id=device, device_id_type=MESH)
    pl.semaphore_wait(barrier, 4)

    issue_in(0)
    tiles = block // TILE
    fill_bias(bias, clip_table, windows, blk * tiles, n_blk * tiles)
    pass_in(0)
    issue_in(1)
    send_halo(0)
    pass_in(1)
    issue_in(2)

    def step(index, carry):
        def run(ahead, action):
            stage = index + ahead

            @pl.when((stage >= 0) & (stage < heads))
            def _():
                action(stage)

        run(1, send_halo)
        run(2, pass_in)
        run(3, issue_in)
        run(0, compute)
        run(-1, finish)
        run(-1, lambda stage: issue_out(stage, range(4)))
        run(-2, lambda stage: pass_out(stage, range(4)))
        return carry

    lax.fori_loop(0, heads + 2, step, 0)

    for array in range(4):
        wait(outs[array], out_recv.at[array])
        wait(sources[array].at[:, pl.ds(0, 3 * heads * HD)], in_send.at[array])
        wait(relay_in.at[array], pass_send.at[array])
        wait(results.at[array, :, pl.ds(0, 3 * tok), :], out_send.at[array])
        wait(relay_out.at[array], back_send.at[array])
    for index in range(2):
        wait(rim_send.at[index], halo_send.at[index])
        wait(rim_send.at[index], rim_send_sem.at[index])


def on_device(n_seq, n_blk, queries, key_states, value_states, grad_out, clip_table, windows):
    tok, width = queries.shape
    heads = width // HD // n_seq
    block = tok * n_seq
    extended = block + 2 * HALO
    low = jnp.bfloat16
    hbm = pl.BlockSpec(memory_space=pl.ANY)
    smem = pl.BlockSpec(memory_space=pltpu.SMEM)
    dma = pltpu.SemaphoreType.DMA
    return pl.pallas_call(
        functools.partial(kernel, "seq", "blk", n_seq, n_blk, heads),
        out_shape=[jax.ShapeDtypeStruct((tok, width), low)] * 4,
        in_specs=[hbm] * 4 + [smem] * 2,
        out_specs=[hbm] * 4,
        scratch_shapes=[
            pltpu.VMEM((2, heads, extended, HD), low),
            pltpu.VMEM((2, heads, block, HD), low),
            pltpu.VMEM((4, heads, tok, HD), low),
            pltpu.VMEM((4, heads, block, HD), low),
            pltpu.VMEM((4, heads, tok, HD), low),
            pltpu.VMEM((2, heads, extended, HD), jnp.float32),
            pltpu.VMEM((2, heads, 2, HALO, HD), low),
            pltpu.VMEM((2, heads, 2, HALO, HD), low),
            pltpu.VMEM((block // TILE, extended), jnp.float32),
            dma((heads, 4)),
            dma((4,)),
            dma((heads, 4)),
            dma((4,)),
            dma((heads, 2, 2)),
            dma((2,)),
            dma((heads, 2, 2)),
            dma((2,)),
            dma((4,)),
            dma((4,)),
            dma((heads, 4)),
            dma((4,)),
        ],
        compiler_params=pltpu.CompilerParams(
            collective_id=0, has_side_effects=True, vmem_limit_bytes=60 * 1024 * 1024
        ),
        name="attention_with_exchange",
    )(queries, key_states, value_states, grad_out, clip_table, windows)


def solution(mesh):
    rows = P(("blk", "seq"), None)
    return jax.shard_map(
        functools.partial(on_device, mesh.shape["seq"], mesh.shape["blk"]),
        mesh=mesh,
        in_specs=(rows, rows, rows, rows, P(), P()),
        out_specs=(rows, rows, rows, rows),
        check_vma=False,
    )
```

```python
import functools
import math

import jax
import jax.numpy as jnp
from jax import lax
from jax.experimental import pallas as pl
from jax.experimental.pallas import tpu as pltpu
from jax.sharding import PartitionSpec as P

HD = 128
TILE = 64
HALO = 448
MASKED = -1e30
PIECE = 32
MESH = pl.DeviceIdType.MESH


def nt(left, right):
    return lax.dot_general(
        left, right, (((1,), (1,)), ((), ())), preferred_element_type=jnp.float32
    )


def nn(left, right):
    return jnp.dot(left, right, preferred_element_type=jnp.float32)


def tn(left, right):
    return lax.dot_general(
        left, right, (((0,), (0,)), ((), ())), preferred_element_type=jnp.float32
    )


def fill_bias(bias, clip_table, windows, first_tile, total_tiles):
    shape = bias.shape
    q_tile = first_tile + lax.broadcasted_iota(jnp.int32, shape, 0)
    k_tile = first_tile - HALO // TILE + (lax.broadcasted_iota(jnp.int32, shape, 1) >> 6)
    none = jnp.full(shape, -1, jnp.int32)
    zero = jnp.zeros(shape, jnp.int32)
    one = jnp.ones(shape, jnp.int32)
    q_clip, k_clip, start = none, none, zero
    rows, cols = one, one
    reach_f, reach_r, reach_c = zero, zero, zero
    for clip in range(clip_table.shape[1]):
        begin = clip_table[0, clip]
        here = q_tile >= begin
        q_clip = jnp.where(here, clip, q_clip)
        k_clip = jnp.where(k_tile >= begin, clip, k_clip)
        start = jnp.where(here, begin, start)
        rows = jnp.where(here, clip_table[2, clip], rows)
        cols = jnp.where(here, clip_table[3, clip], cols)
        reach_f = jnp.where(here, windows[0, clip], reach_f)
        reach_r = jnp.where(here, windows[1, clip], reach_r)
        reach_c = jnp.where(here, windows[2, clip], reach_c)

    def place(tile):
        local = tile - start
        line = jnp.where(cols == 2, local >> 1, local)
        frame = jnp.where(rows == 2, line >> 1, line)
        return frame, line - frame * rows, local - line * cols

    q_frame, q_row, q_col = place(q_tile)
    k_frame, k_row, k_col = place(k_tile)
    allowed = (
        (q_clip == k_clip)
        & (k_tile >= 0)
        & (k_tile < total_tiles)
        & (jnp.abs(q_frame - k_frame) <= reach_f)
        & (jnp.abs(q_row - k_row) <= reach_r)
        & (jnp.abs(q_col - k_col) <= reach_c)
    )
    bias[...] = jnp.where(allowed, 0.0, MASKED).astype(jnp.float32)


def kernel(
    seq_axis,
    blk_axis,
    n_seq,
    n_blk,
    heads,
    q_in,
    k_in,
    v_in,
    g_in,
    clip_table,
    windows,
    att_out,
    dq_out,
    dk_out,
    dv_out,
    kv,
    qg,
    relay_in,
    results,
    relay_out,
    acc,
    rim_send,
    rim_recv,
    bias,
    in_recv,
    in_send,
    hop_recv,
    pass_send,
    halo_recv,
    halo_send,
    rim_recv_sem,
    rim_send_sem,
    out_recv,
    out_send,
    back_recv,
    back_send,
):
    scale = 1.0 / math.sqrt(HD)
    tok = q_in.shape[0]
    block = tok * n_seq
    me = lax.axis_index(seq_axis)
    blk = lax.axis_index(blk_axis)
    right = lax.rem(me + 1, n_seq)
    left = lax.rem(me + n_seq - 1, n_seq)
    far = lax.rem(me + 2, n_seq)
    above = lax.rem(blk + 1, n_blk)
    below = lax.rem(blk + n_blk - 1, n_blk)
    to_right, to_left = {seq_axis: right}, {seq_axis: left}
    to_above, to_below = {blk_axis: above}, {blk_axis: below}

    sources = (k_in, v_in, q_in, g_in)
    outs = (att_out, dq_out, dk_out, dv_out)

    def landing(array, stage, origin):
        row = origin * tok
        if array < 2:
            return kv.at[array, stage, pl.ds(HALO + row, tok), :]
        return qg.at[array - 2, stage, pl.ds(row, tok), :]

    def columns(ref, owner, stage):
        start = pl.multiple_of((owner * heads + stage) * HD, HD)
        return ref.at[:, pl.ds(start, HD)]

    def send(src, dst, send_sem, recv_sem, device):
        pltpu.make_async_remote_copy(
            src_ref=src,
            dst_ref=dst,
            send_sem=send_sem,
            recv_sem=recv_sem,
            device_id=device,
            device_id_type=MESH,
        ).start()

    def wait(ref, sem):
        pltpu.make_async_copy(ref, ref, sem).wait()

    def issue_in(stage):
        for array, src in enumerate(sources):
            via = to_right if array % 2 == 0 else to_left
            send(
                columns(src, far, stage),
                relay_in.at[array, stage],
                in_send.at[array],
                hop_recv.at[stage, array],
                via,
            )
        for array, src in enumerate(sources):
            arrived = in_recv.at[stage, array]
            sent = in_send.at[array]
            send(columns(src, right, stage), landing(array, stage, me), sent, arrived, to_right)
            send(columns(src, left, stage), landing(array, stage, me), sent, arrived, to_left)
            pltpu.make_async_copy(
                columns(src, me, stage), landing(array, stage, me), arrived
            ).start()

    def pass_in(stage):
        for array in range(4):
            wait(relay_in.at[array, stage], hop_recv.at[stage, array])
            onward, origin = (to_right, left) if array % 2 == 0 else (to_left, right)
            send(
                relay_in.at[array, stage],
                landing(array, stage, origin),
                pass_send.at[array],
                in_recv.at[stage, array],
                onward,
            )

    def send_halo(stage):
        for array in range(2):
            wait(kv.at[array, stage, pl.ds(HALO, block), :], in_recv.at[stage, array])
            sent = halo_send.at[array]
            send(
                kv.at[array, stage, pl.ds(block, HALO), :],
                kv.at[array, stage, pl.ds(0, HALO), :],
                sent,
                halo_recv.at[stage, array, 0],
                to_above,
            )
            send(
                kv.at[array, stage, pl.ds(HALO, HALO), :],
                kv.at[array, stage, pl.ds(HALO + block, HALO), :],
                sent,
                halo_recv.at[stage, array, 1],
                to_below,
            )

    def compute(stage):
        for array in range(2):
            wait(qg.at[array, stage], in_recv.at[stage, 2 + array])
            wait(kv.at[array, stage, pl.ds(0, HALO), :], halo_recv.at[stage, array, 0])
            wait(kv.at[array, stage, pl.ds(HALO + block, HALO), :], halo_recv.at[stage, array, 1])
        rows = block // 2
        span = rows + 2 * HALO
        for part in range(2):
            low = part * rows
            q = qg[0, stage, low : low + rows, :]
            g = qg[1, stage, low : low + rows, :]
            k = kv[0, stage, low : low + span, :]
            v = kv[1, stage, low : low + span, :]
            product = nt(q, k)
            per_part = rows // TILE
            scores = jnp.concatenate(
                [
                    product[t * TILE : (t + 1) * TILE] * scale
                    + bias[part * per_part + t : part * per_part + t + 1, low : low + span]
                    for t in range(per_part)
                ],
                axis=0,
            )
            row_max = jnp.max(scores, axis=1, keepdims=True)
            weights = jnp.exp(scores - row_max)
            total = jnp.sum(weights, axis=1, keepdims=True)
            probs = weights * (1.0 / total)
            probs_low = probs.astype(jnp.bfloat16)
            attended = nn(probs_low, v).astype(jnp.bfloat16)
            delta = jnp.sum(
                g.astype(jnp.float32) * attended.astype(jnp.float32), axis=1, keepdims=True
            )
            dscores = (probs * (nt(g, v) - delta) * scale).astype(jnp.bfloat16)
            results[0, stage, low : low + rows, :] = attended
            results[1, stage, low : low + rows, :] = nn(dscores, k).astype(jnp.bfloat16)
            for index, grad in enumerate((tn(dscores, q), tn(probs_low, g))):
                if part == 0:
                    acc[index, stage, 0:span, :] = grad
                else:
                    shared = span - rows
                    acc[index, stage, rows:span, :] += grad[:shared]
                    acc[index, stage, span : span + rows, :] = grad[shared:]
        for index in range(2):
            rim_send[index, stage, 0] = acc[index, stage, 0:HALO, :].astype(jnp.bfloat16)
            rim_send[index, stage, 1] = acc[
                index, stage, HALO + block : 2 * HALO + block, :
            ].astype(jnp.bfloat16)
            sent = rim_send_sem.at[index]
            send(
                rim_send.at[index, stage, 0],
                rim_recv.at[index, stage, 1],
                sent,
                rim_recv_sem.at[stage, index, 1],
                to_below,
            )
            send(
                rim_send.at[index, stage, 1],
                rim_recv.at[index, stage, 0],
                sent,
                rim_recv_sem.at[stage, index, 0],
                to_above,
            )

    def finish(stage):
        for index in range(2):
            wait(rim_recv.at[index, stage, 0], rim_recv_sem.at[stage, index, 0])
            wait(rim_recv.at[index, stage, 1], rim_recv_sem.at[stage, index, 1])
            edge = block - HALO
            acc[index, stage, HALO : 2 * HALO, :] += rim_recv[index, stage, 0].astype(jnp.float32)
            acc[index, stage, HALO + edge : HALO + block, :] += rim_recv[index, stage, 1].astype(
                jnp.float32
            )
            results[2 + index, stage] = acc[index, stage, HALO : HALO + block, :].astype(
                jnp.bfloat16
            )

    def rows_of(array, stage, owner):
        return results.at[array, stage, pl.ds(pl.multiple_of(owner * tok, tok), tok), :]

    def issue_out(stage, arrays):
        for array in arrays:
            via = to_right if array % 2 == 0 else to_left
            send(
                rows_of(array, stage, far),
                relay_out.at[array, stage],
                out_send.at[array],
                back_recv.at[stage, array],
                via,
            )
        for array in arrays:
            arrived = out_recv.at[array]
            sent = out_send.at[array]
            mine = columns(outs[array], me, stage)
            send(rows_of(array, stage, right), mine, sent, arrived, to_right)
            send(rows_of(array, stage, left), mine, sent, arrived, to_left)
            pltpu.make_async_copy(rows_of(array, stage, me), mine, arrived).start()

    def pass_out(stage, arrays):
        for array in arrays:
            wait(relay_out.at[array, stage], back_recv.at[stage, array])
            onward, origin = (to_right, left) if array % 2 == 0 else (to_left, right)
            send(
                relay_out.at[array, stage],
                columns(outs[array], origin, stage),
                back_send.at[array],
                out_recv.at[array],
                onward,
            )

    barrier = pltpu.get_barrier_semaphore()
    for device in (to_right, to_left, to_above, to_below):
        pl.semaphore_signal(barrier, inc=1, device_id=device, device_id_type=MESH)
    pl.semaphore_wait(barrier, 4)

    issue_in(0)
    tiles = block // TILE
    fill_bias(bias, clip_table, windows, blk * tiles, n_blk * tiles)
    pass_in(0)
    issue_in(1)
    send_halo(0)
    pass_in(1)
    issue_in(2)

    def step(index, carry):
        def run(ahead, action):
            stage = index + ahead

            @pl.when((stage >= 0) & (stage < heads))
            def _():
                action(stage)

        run(1, send_halo)
        run(2, pass_in)
        run(3, issue_in)
        run(0, compute)
        run(-1, finish)
        run(-1, lambda stage: issue_out(stage, range(4)))
        run(-2, lambda stage: pass_out(stage, range(4)))
        return carry

    lax.fori_loop(0, heads + 2, step, 0)

    for array in range(4):
        wait(outs[array], out_recv.at[array])
        wait(sources[array].at[:, pl.ds(0, 3 * heads * HD)], in_send.at[array])
        wait(relay_in.at[array], pass_send.at[array])
        wait(results.at[array, :, pl.ds(0, 3 * tok), :], out_send.at[array])
        wait(relay_out.at[array], back_send.at[array])
    for index in range(2):
        wait(rim_send.at[index], halo_send.at[index])
        wait(rim_send.at[index], rim_send_sem.at[index])


def hand_over(*refs):
    inner, outer, held, (arrived, left) = refs[:4], refs[4:8], refs[8], refs[9:]
    tok = held.shape[1]
    pieces = [(array, row) for row in range(0, tok, PIECE) for array in range(4)]

    def take(array, row):
        rows = pl.ds(row, PIECE)
        return pltpu.make_async_copy(
            inner[array].at[rows], held.at[array, rows], arrived.at[array, row // PIECE]
        )

    def put(array, row):
        rows = pl.ds(row, PIECE)
        return pltpu.make_async_copy(
            held.at[array, rows], outer[array].at[rows], left.at[array, row // PIECE]
        )

    for piece in pieces:
        take(*piece).start()
    for piece in pieces:
        take(*piece).wait()
        put(*piece).start()
    for piece in pieces:
        put(*piece).wait()


def on_device(n_seq, n_blk, queries, key_states, value_states, grad_out, clip_table, windows):
    tok, width = queries.shape
    heads = width // HD // n_seq
    block = tok * n_seq
    extended = block + 2 * HALO
    low = jnp.bfloat16
    hbm = pl.BlockSpec(memory_space=pl.ANY)
    smem = pl.BlockSpec(memory_space=pltpu.SMEM)
    dma = pltpu.SemaphoreType.DMA
    inner = pl.pallas_call(
        functools.partial(kernel, "seq", "blk", n_seq, n_blk, heads),
        out_shape=[jax.ShapeDtypeStruct((tok, width), low)] * 4,
        in_specs=[hbm] * 4 + [smem] * 2,
        out_specs=[hbm] * 4,
        scratch_shapes=[
            pltpu.VMEM((2, heads, extended, HD), low),
            pltpu.VMEM((2, heads, block, HD), low),
            pltpu.VMEM((4, heads, tok, HD), low),
            pltpu.VMEM((4, heads, block, HD), low),
            pltpu.VMEM((4, heads, tok, HD), low),
            pltpu.VMEM((2, heads, extended, HD), jnp.float32),
            pltpu.VMEM((2, heads, 2, HALO, HD), low),
            pltpu.VMEM((2, heads, 2, HALO, HD), low),
            pltpu.VMEM((block // TILE, extended), jnp.float32),
            dma((heads, 4)),
            dma((4,)),
            dma((heads, 4)),
            dma((4,)),
            dma((heads, 2, 2)),
            dma((2,)),
            dma((heads, 2, 2)),
            dma((2,)),
            dma((4,)),
            dma((4,)),
            dma((heads, 4)),
            dma((4,)),
        ],
        compiler_params=pltpu.CompilerParams(
            collective_id=0, has_side_effects=True, vmem_limit_bytes=60 * 1024 * 1024
        ),
        name="attention_with_exchange",
    )(queries, key_states, value_states, grad_out, clip_table.T, windows.T)
    return pl.pallas_call(
        hand_over,
        out_shape=[jax.ShapeDtypeStruct((tok, width), low)] * 4,
        in_specs=[hbm] * 4,
        out_specs=[hbm] * 4,
        scratch_shapes=[
            pltpu.VMEM((4, tok, width), low),
            dma((4, tok // PIECE)),
            dma((4, tok // PIECE)),
        ],
        name="hand_over",
    )(*inner)


def solution(mesh):
    rows = P(("blk", "seq"), None)
    return jax.shard_map(
        functools.partial(on_device, mesh.shape["seq"], mesh.shape["blk"]),
        mesh=mesh,
        in_specs=(rows, rows, rows, rows, P(), P()),
        out_specs=(rows, rows, rows, rows),
        check_vma=False,
    )
```

```python
import functools
import math

import jax
import jax.numpy as jnp
from jax import lax
from jax.experimental import pallas as pl
from jax.experimental.pallas import tpu as pltpu
from jax.sharding import PartitionSpec as P

HD = 128
TILE = 64
HALO = 448
MASKED = -1e30
PIECE = 32
MESH = pl.DeviceIdType.MESH


def nt(left, right):
    return lax.dot_general(
        left, right, (((1,), (1,)), ((), ())), preferred_element_type=jnp.float32
    )


def nn(left, right):
    return jnp.dot(left, right, preferred_element_type=jnp.float32)


def tn(left, right):
    return lax.dot_general(
        left, right, (((0,), (0,)), ((), ())), preferred_element_type=jnp.float32
    )


def fill_bias(bias, clip_table, windows, first_tile, total_tiles):
    shape = bias.shape
    q_tile = first_tile + lax.broadcasted_iota(jnp.int32, shape, 0)
    k_tile = first_tile - HALO // TILE + (lax.broadcasted_iota(jnp.int32, shape, 1) >> 6)
    none = jnp.full(shape, -1, jnp.int32)
    zero = jnp.zeros(shape, jnp.int32)
    one = jnp.ones(shape, jnp.int32)
    q_clip, k_clip, start = none, none, zero
    rows, cols = one, one
    reach_f, reach_r, reach_c = zero, zero, zero
    for clip in range(clip_table.shape[1]):
        begin = clip_table[0, clip]
        here = q_tile >= begin
        q_clip = jnp.where(here, clip, q_clip)
        k_clip = jnp.where(k_tile >= begin, clip, k_clip)
        start = jnp.where(here, begin, start)
        rows = jnp.where(here, clip_table[2, clip], rows)
        cols = jnp.where(here, clip_table[3, clip], cols)
        reach_f = jnp.where(here, windows[0, clip], reach_f)
        reach_r = jnp.where(here, windows[1, clip], reach_r)
        reach_c = jnp.where(here, windows[2, clip], reach_c)

    def place(tile):
        local = tile - start
        line = jnp.where(cols == 2, local >> 1, local)
        frame = jnp.where(rows == 2, line >> 1, line)
        return frame, line - frame * rows, local - line * cols

    q_frame, q_row, q_col = place(q_tile)
    k_frame, k_row, k_col = place(k_tile)
    allowed = (
        (q_clip == k_clip)
        & (k_tile >= 0)
        & (k_tile < total_tiles)
        & (jnp.abs(q_frame - k_frame) <= reach_f)
        & (jnp.abs(q_row - k_row) <= reach_r)
        & (jnp.abs(q_col - k_col) <= reach_c)
    )
    bias[...] = jnp.where(allowed, 0.0, MASKED).astype(jnp.float32)


def kernel(
    seq_axis,
    blk_axis,
    n_seq,
    n_blk,
    heads,
    q_in,
    k_in,
    v_in,
    g_in,
    clip_table,
    windows,
    att_out,
    dq_out,
    dk_out,
    dv_out,
    kv,
    qg,
    relay_in,
    results,
    relay_out,
    acc,
    rim_send,
    rim_recv,
    bias,
    in_recv,
    in_send,
    hop_recv,
    pass_send,
    halo_recv,
    halo_send,
    rim_recv_sem,
    rim_send_sem,
    out_recv,
    out_send,
    back_recv,
    back_send,
):
    scale = 1.0 / math.sqrt(HD)
    tok = q_in.shape[0]
    block = tok * n_seq
    me = lax.axis_index(seq_axis)
    blk = lax.axis_index(blk_axis)
    right = lax.rem(me + 1, n_seq)
    left = lax.rem(me + n_seq - 1, n_seq)
    far = lax.rem(me + 2, n_seq)
    above = lax.rem(blk + 1, n_blk)
    below = lax.rem(blk + n_blk - 1, n_blk)
    to_right, to_left = {seq_axis: right}, {seq_axis: left}
    to_above, to_below = {blk_axis: above}, {blk_axis: below}

    sources = (k_in, v_in, q_in, g_in)
    outs = (att_out, dq_out, dk_out, dv_out)

    def landing(array, stage, origin):
        row = origin * tok
        if array < 2:
            return kv.at[array, stage, pl.ds(HALO + row, tok), :]
        return qg.at[array - 2, stage, pl.ds(row, tok), :]

    def columns(ref, owner, stage):
        start = pl.multiple_of((owner * heads + stage) * HD, HD)
        return ref.at[:, pl.ds(start, HD)]

    def send(src, dst, send_sem, recv_sem, device):
        pltpu.make_async_remote_copy(
            src_ref=src,
            dst_ref=dst,
            send_sem=send_sem,
            recv_sem=recv_sem,
            device_id=device,
            device_id_type=MESH,
        ).start()

    def wait(ref, sem):
        pltpu.make_async_copy(ref, ref, sem).wait()

    def issue_in(stage):
        for array, src in enumerate(sources):
            via = to_right if array % 2 == 0 else to_left
            send(
                columns(src, far, stage),
                relay_in.at[array, stage],
                in_send.at[array],
                hop_recv.at[stage, array],
                via,
            )
        for array, src in enumerate(sources):
            arrived = in_recv.at[stage, array]
            sent = in_send.at[array]
            send(columns(src, right, stage), landing(array, stage, me), sent, arrived, to_right)
            send(columns(src, left, stage), landing(array, stage, me), sent, arrived, to_left)
            pltpu.make_async_copy(
                columns(src, me, stage), landing(array, stage, me), arrived
            ).start()

    def pass_in(stage):
        for array in range(4):
            wait(relay_in.at[array, stage], hop_recv.at[stage, array])
            onward, origin = (to_right, left) if array % 2 == 0 else (to_left, right)
            send(
                relay_in.at[array, stage],
                landing(array, stage, origin),
                pass_send.at[array],
                in_recv.at[stage, array],
                onward,
            )

    def send_halo(stage):
        for array in range(2):
            wait(kv.at[array, stage, pl.ds(HALO, block), :], in_recv.at[stage, array])
            sent = halo_send.at[array]
            send(
                kv.at[array, stage, pl.ds(block, HALO), :],
                kv.at[array, stage, pl.ds(0, HALO), :],
                sent,
                halo_recv.at[stage, array, 0],
                to_above,
            )
            send(
                kv.at[array, stage, pl.ds(HALO, HALO), :],
                kv.at[array, stage, pl.ds(HALO + block, HALO), :],
                sent,
                halo_recv.at[stage, array, 1],
                to_below,
            )

    def compute(stage, between):
        for array in range(2):
            wait(qg.at[array, stage], in_recv.at[stage, 2 + array])
            wait(kv.at[array, stage, pl.ds(0, HALO), :], halo_recv.at[stage, array, 0])
            wait(kv.at[array, stage, pl.ds(HALO + block, HALO), :], halo_recv.at[stage, array, 1])
        rows = block // 2
        span = rows + 2 * HALO
        for part in range(2):
            if part == 1:
                between()
            low = part * rows
            q = qg[0, stage, low : low + rows, :]
            g = qg[1, stage, low : low + rows, :]
            k = kv[0, stage, low : low + span, :]
            v = kv[1, stage, low : low + span, :]
            product = nt(q, k)
            per_part = rows // TILE
            scores = jnp.concatenate(
                [
                    product[t * TILE : (t + 1) * TILE] * scale
                    + bias[part * per_part + t : part * per_part + t + 1, low : low + span]
                    for t in range(per_part)
                ],
                axis=0,
            )
            row_max = jnp.max(scores, axis=1, keepdims=True)
            weights = jnp.exp(scores - row_max)
            total = jnp.sum(weights, axis=1, keepdims=True)
            probs = weights * (1.0 / total)
            probs_low = probs.astype(jnp.bfloat16)
            attended = nn(probs_low, v).astype(jnp.bfloat16)
            delta = jnp.sum(
                g.astype(jnp.float32) * attended.astype(jnp.float32), axis=1, keepdims=True
            )
            dscores = (probs * (nt(g, v) - delta) * scale).astype(jnp.bfloat16)
            results[0, stage, low : low + rows, :] = attended
            results[1, stage, low : low + rows, :] = nn(dscores, k).astype(jnp.bfloat16)
            for index, grad in enumerate((tn(dscores, q), tn(probs_low, g))):
                if part == 0:
                    acc[index, stage, 0:span, :] = grad
                else:
                    shared = span - rows
                    acc[index, stage, rows:span, :] += grad[:shared]
                    acc[index, stage, span : span + rows, :] = grad[shared:]
        for index in range(2):
            rim_send[index, stage, 0] = acc[index, stage, 0:HALO, :].astype(jnp.bfloat16)
            rim_send[index, stage, 1] = acc[
                index, stage, HALO + block : 2 * HALO + block, :
            ].astype(jnp.bfloat16)
            sent = rim_send_sem.at[index]
            send(
                rim_send.at[index, stage, 0],
                rim_recv.at[index, stage, 1],
                sent,
                rim_recv_sem.at[stage, index, 1],
                to_below,
            )
            send(
                rim_send.at[index, stage, 1],
                rim_recv.at[index, stage, 0],
                sent,
                rim_recv_sem.at[stage, index, 0],
                to_above,
            )

    def finish(stage):
        for index in range(2):
            wait(rim_recv.at[index, stage, 0], rim_recv_sem.at[stage, index, 0])
            wait(rim_recv.at[index, stage, 1], rim_recv_sem.at[stage, index, 1])
            edge = block - HALO
            acc[index, stage, HALO : 2 * HALO, :] += rim_recv[index, stage, 0].astype(jnp.float32)
            acc[index, stage, HALO + edge : HALO + block, :] += rim_recv[index, stage, 1].astype(
                jnp.float32
            )
            results[2 + index, stage] = acc[index, stage, HALO : HALO + block, :].astype(
                jnp.bfloat16
            )

    def rows_of(array, stage, owner):
        return results.at[array, stage, pl.ds(pl.multiple_of(owner * tok, tok), tok), :]

    def issue_out(stage, arrays):
        for array in arrays:
            via = to_right if array % 2 == 0 else to_left
            send(
                rows_of(array, stage, far),
                relay_out.at[array, stage],
                out_send.at[array],
                back_recv.at[stage, array],
                via,
            )
        for array in arrays:
            arrived = out_recv.at[array]
            sent = out_send.at[array]
            mine = columns(outs[array], me, stage)
            send(rows_of(array, stage, right), mine, sent, arrived, to_right)
            send(rows_of(array, stage, left), mine, sent, arrived, to_left)
            pltpu.make_async_copy(rows_of(array, stage, me), mine, arrived).start()

    def pass_out(stage, arrays):
        for array in arrays:
            wait(relay_out.at[array, stage], back_recv.at[stage, array])
            onward, origin = (to_right, left) if array % 2 == 0 else (to_left, right)
            send(
                relay_out.at[array, stage],
                columns(outs[array], origin, stage),
                back_send.at[array],
                out_recv.at[array],
                onward,
            )

    barrier = pltpu.get_barrier_semaphore()
    for device in (to_right, to_left, to_above, to_below):
        pl.semaphore_signal(barrier, inc=1, device_id=device, device_id_type=MESH)
    pl.semaphore_wait(barrier, 4)

    issue_in(0)
    tiles = block // TILE
    fill_bias(bias, clip_table, windows, blk * tiles, n_blk * tiles)
    pass_in(0)
    issue_in(1)
    send_halo(0)
    pass_in(1)
    issue_in(2)

    def step(index, carry):
        def run(ahead, action):
            stage = index + ahead

            @pl.when((stage >= 0) & (stage < heads))
            def _():
                action(stage)

        def arrivals():
            run(1, send_halo)
            run(2, pass_in)
            run(3, issue_in)

        run(0, lambda stage: compute(stage, arrivals))
        run(0, lambda stage: issue_out(stage, (0, 1)))
        run(-2, lambda stage: pass_out(stage, (0, 1)))
        run(-1, finish)
        run(-1, lambda stage: issue_out(stage, (2, 3)))
        run(-2, lambda stage: pass_out(stage, (2, 3)))
        return carry

    lax.fori_loop(0, heads + 2, step, 0)

    for array in range(4):
        wait(outs[array], out_recv.at[array])
        wait(sources[array].at[:, pl.ds(0, 3 * heads * HD)], in_send.at[array])
        wait(relay_in.at[array], pass_send.at[array])
        wait(results.at[array, :, pl.ds(0, 3 * tok), :], out_send.at[array])
        wait(relay_out.at[array], back_send.at[array])
    for index in range(2):
        wait(rim_send.at[index], halo_send.at[index])
        wait(rim_send.at[index], rim_send_sem.at[index])


def hand_over(*refs):
    inner, outer, held, (arrived, left) = refs[:4], refs[4:8], refs[8], refs[9:]
    tok = held.shape[1]
    pieces = [(array, row) for row in range(0, tok, PIECE) for array in range(4)]

    def take(array, row):
        rows = pl.ds(row, PIECE)
        return pltpu.make_async_copy(
            inner[array].at[rows], held.at[array, rows], arrived.at[array, row // PIECE]
        )

    def put(array, row):
        rows = pl.ds(row, PIECE)
        return pltpu.make_async_copy(
            held.at[array, rows], outer[array].at[rows], left.at[array, row // PIECE]
        )

    for piece in pieces:
        take(*piece).start()
    for piece in pieces:
        take(*piece).wait()
        put(*piece).start()
    for piece in pieces:
        put(*piece).wait()


def on_device(n_seq, n_blk, queries, key_states, value_states, grad_out, clip_table, windows):
    tok, width = queries.shape
    heads = width // HD // n_seq
    block = tok * n_seq
    extended = block + 2 * HALO
    low = jnp.bfloat16
    hbm = pl.BlockSpec(memory_space=pl.ANY)
    smem = pl.BlockSpec(memory_space=pltpu.SMEM)
    dma = pltpu.SemaphoreType.DMA
    inner = pl.pallas_call(
        functools.partial(kernel, "seq", "blk", n_seq, n_blk, heads),
        out_shape=[jax.ShapeDtypeStruct((tok, width), low)] * 4,
        in_specs=[hbm] * 4 + [smem] * 2,
        out_specs=[hbm] * 4,
        scratch_shapes=[
            pltpu.VMEM((2, heads, extended, HD), low),
            pltpu.VMEM((2, heads, block, HD), low),
            pltpu.VMEM((4, heads, tok, HD), low),
            pltpu.VMEM((4, heads, block, HD), low),
            pltpu.VMEM((4, heads, tok, HD), low),
            pltpu.VMEM((2, heads, extended, HD), jnp.float32),
            pltpu.VMEM((2, heads, 2, HALO, HD), low),
            pltpu.VMEM((2, heads, 2, HALO, HD), low),
            pltpu.VMEM((block // TILE, extended), jnp.float32),
            dma((heads, 4)),
            dma((4,)),
            dma((heads, 4)),
            dma((4,)),
            dma((heads, 2, 2)),
            dma((2,)),
            dma((heads, 2, 2)),
            dma((2,)),
            dma((4,)),
            dma((4,)),
            dma((heads, 4)),
            dma((4,)),
        ],
        compiler_params=pltpu.CompilerParams(
            collective_id=0, has_side_effects=True, vmem_limit_bytes=60 * 1024 * 1024
        ),
        name="attention_with_exchange",
    )(queries, key_states, value_states, grad_out, clip_table.T, windows.T)
    return pl.pallas_call(
        hand_over,
        out_shape=[jax.ShapeDtypeStruct((tok, width), low)] * 4,
        in_specs=[hbm] * 4,
        out_specs=[hbm] * 4,
        scratch_shapes=[
            pltpu.VMEM((4, tok, width), low),
            dma((4, tok // PIECE)),
            dma((4, tok // PIECE)),
        ],
        name="hand_over",
    )(*inner)


def solution(mesh):
    rows = P(("blk", "seq"), None)
    return jax.shard_map(
        functools.partial(on_device, mesh.shape["seq"], mesh.shape["blk"]),
        mesh=mesh,
        in_specs=(rows, rows, rows, rows, P(), P()),
        out_specs=(rows, rows, rows, rows),
        check_vma=False,
    )
```

```python
import functools
import math

import jax
import jax.numpy as jnp
from jax import lax
from jax.experimental import pallas as pl
from jax.experimental.pallas import tpu as pltpu
from jax.sharding import PartitionSpec as P

HD = 128
TILE = 64
HALO = 448
MASKED = -1e30
PIECE = 32
MESH = pl.DeviceIdType.MESH


def nt(left, right):
    return lax.dot_general(
        left, right, (((1,), (1,)), ((), ())), preferred_element_type=jnp.float32
    )


def nn(left, right):
    return jnp.dot(left, right, preferred_element_type=jnp.float32)


def tn(left, right):
    return lax.dot_general(
        left, right, (((0,), (0,)), ((), ())), preferred_element_type=jnp.float32
    )


def fill_bias(bias, clip_table, windows, first_tile, total_tiles):
    shape = bias.shape
    q_tile = first_tile + lax.broadcasted_iota(jnp.int32, shape, 0)
    k_tile = first_tile - HALO // TILE + (lax.broadcasted_iota(jnp.int32, shape, 1) >> 6)
    none = jnp.full(shape, -1, jnp.int32)
    zero = jnp.zeros(shape, jnp.int32)
    one = jnp.ones(shape, jnp.int32)
    q_clip, k_clip, start = none, none, zero
    rows, cols = one, one
    reach_f, reach_r, reach_c = zero, zero, zero
    for clip in range(clip_table.shape[1]):
        begin = clip_table[0, clip]
        here = q_tile >= begin
        q_clip = jnp.where(here, clip, q_clip)
        k_clip = jnp.where(k_tile >= begin, clip, k_clip)
        start = jnp.where(here, begin, start)
        rows = jnp.where(here, clip_table[2, clip], rows)
        cols = jnp.where(here, clip_table[3, clip], cols)
        reach_f = jnp.where(here, windows[0, clip], reach_f)
        reach_r = jnp.where(here, windows[1, clip], reach_r)
        reach_c = jnp.where(here, windows[2, clip], reach_c)

    def place(tile):
        local = tile - start
        line = jnp.where(cols == 2, local >> 1, local)
        frame = jnp.where(rows == 2, line >> 1, line)
        return frame, line - frame * rows, local - line * cols

    q_frame, q_row, q_col = place(q_tile)
    k_frame, k_row, k_col = place(k_tile)
    allowed = (
        (q_clip == k_clip)
        & (k_tile >= 0)
        & (k_tile < total_tiles)
        & (jnp.abs(q_frame - k_frame) <= reach_f)
        & (jnp.abs(q_row - k_row) <= reach_r)
        & (jnp.abs(q_col - k_col) <= reach_c)
    )
    bias[...] = jnp.where(allowed, 0.0, MASKED).astype(jnp.float32)


def kernel(
    seq_axis,
    blk_axis,
    n_seq,
    n_blk,
    heads,
    q_in,
    k_in,
    v_in,
    g_in,
    clip_table,
    windows,
    att_out,
    dq_out,
    dk_out,
    dv_out,
    kv,
    qg,
    relay_in,
    results,
    relay_out,
    acc,
    rim_send,
    rim_recv,
    bias,
    in_recv,
    in_send,
    hop_recv,
    pass_send,
    halo_recv,
    halo_send,
    rim_recv_sem,
    rim_send_sem,
    out_recv,
    out_send,
    back_recv,
    back_send,
):
    scale = 1.0 / math.sqrt(HD)
    tok = q_in.shape[0]
    block = tok * n_seq
    me = lax.axis_index(seq_axis)
    blk = lax.axis_index(blk_axis)
    right = lax.rem(me + 1, n_seq)
    left = lax.rem(me + n_seq - 1, n_seq)
    far = lax.rem(me + 2, n_seq)
    above = lax.rem(blk + 1, n_blk)
    below = lax.rem(blk + n_blk - 1, n_blk)
    to_right, to_left = {seq_axis: right}, {seq_axis: left}
    to_above, to_below = {blk_axis: above}, {blk_axis: below}

    sources = (k_in, v_in, q_in, g_in)
    outs = (att_out, dq_out, dk_out, dv_out)

    def landing(array, stage, origin):
        row = origin * tok
        if array < 2:
            return kv.at[array, stage, pl.ds(HALO + row, tok), :]
        return qg.at[array - 2, stage, pl.ds(row, tok), :]

    def columns(ref, owner, stage):
        start = pl.multiple_of((owner * heads + stage) * HD, HD)
        return ref.at[:, pl.ds(start, HD)]

    def send(src, dst, send_sem, recv_sem, device):
        pltpu.make_async_remote_copy(
            src_ref=src,
            dst_ref=dst,
            send_sem=send_sem,
            recv_sem=recv_sem,
            device_id=device,
            device_id_type=MESH,
        ).start()

    def wait(ref, sem):
        pltpu.make_async_copy(ref, ref, sem).wait()

    def issue_in(stage):
        for array, src in enumerate(sources):
            via = to_right if array % 2 == 0 else to_left
            send(
                columns(src, far, stage),
                relay_in.at[array, stage],
                in_send.at[array],
                hop_recv.at[stage, array],
                via,
            )
        for array, src in enumerate(sources):
            arrived = in_recv.at[stage, array]
            sent = in_send.at[array]
            send(columns(src, right, stage), landing(array, stage, me), sent, arrived, to_right)
            send(columns(src, left, stage), landing(array, stage, me), sent, arrived, to_left)
            pltpu.make_async_copy(
                columns(src, me, stage), landing(array, stage, me), arrived
            ).start()

    def pass_in(stage):
        for array in range(4):
            wait(relay_in.at[array, stage], hop_recv.at[stage, array])
            onward, origin = (to_right, left) if array % 2 == 0 else (to_left, right)
            send(
                relay_in.at[array, stage],
                landing(array, stage, origin),
                pass_send.at[array],
                in_recv.at[stage, array],
                onward,
            )

    def send_halo(stage):
        for array in range(2):
            wait(kv.at[array, stage, pl.ds(HALO, block), :], in_recv.at[stage, array])
            sent = halo_send.at[array]
            send(
                kv.at[array, stage, pl.ds(block, HALO), :],
                kv.at[array, stage, pl.ds(0, HALO), :],
                sent,
                halo_recv.at[stage, array, 0],
                to_above,
            )
            send(
                kv.at[array, stage, pl.ds(HALO, HALO), :],
                kv.at[array, stage, pl.ds(HALO + block, HALO), :],
                sent,
                halo_recv.at[stage, array, 1],
                to_below,
            )

    def compute(stage):
        for array in range(2):
            wait(qg.at[array, stage], in_recv.at[stage, 2 + array])
            wait(kv.at[array, stage, pl.ds(0, HALO), :], halo_recv.at[stage, array, 0])
            wait(kv.at[array, stage, pl.ds(HALO + block, HALO), :], halo_recv.at[stage, array, 1])
        rows = block // 2
        span = rows + 2 * HALO
        for part in range(2):
            low = part * rows
            q = qg[0, stage, low : low + rows, :]
            g = qg[1, stage, low : low + rows, :]
            k = kv[0, stage, low : low + span, :]
            v = kv[1, stage, low : low + span, :]
            product = nt(q, k)
            per_part = rows // TILE
            scores = jnp.concatenate(
                [
                    product[t * TILE : (t + 1) * TILE]
                    + bias[part * per_part + t : part * per_part + t + 1, low : low + span]
                    for t in range(per_part)
                ],
                axis=0,
            )
            row_max = jnp.max(scores, axis=1, keepdims=True)
            weights = jnp.exp2((scores - row_max) * (scale * math.log2(math.e)))
            total = jnp.sum(weights, axis=1, keepdims=True)
            probs = weights * (1.0 / total)
            probs_low = probs.astype(jnp.bfloat16)
            attended = nn(probs_low, v).astype(jnp.bfloat16)
            delta = jnp.sum(
                g.astype(jnp.float32) * attended.astype(jnp.float32), axis=1, keepdims=True
            )
            dscores = (probs * (nt(g, v) - delta)).astype(jnp.bfloat16)
            results[0, stage, low : low + rows, :] = attended
            results[1, stage, low : low + rows, :] = (nn(dscores, k) * scale).astype(jnp.bfloat16)
            for index, grad in enumerate((tn(dscores, q) * scale, tn(probs_low, g))):
                if part == 0:
                    acc[index, stage, 0:span, :] = grad
                else:
                    shared = span - rows
                    acc[index, stage, rows:span, :] += grad[:shared]
                    acc[index, stage, span : span + rows, :] = grad[shared:]
        for index in range(2):
            rim_send[index, stage, 0] = acc[index, stage, 0:HALO, :].astype(jnp.bfloat16)
            rim_send[index, stage, 1] = acc[
                index, stage, HALO + block : 2 * HALO + block, :
            ].astype(jnp.bfloat16)
            sent = rim_send_sem.at[index]
            send(
                rim_send.at[index, stage, 0],
                rim_recv.at[index, stage, 1],
                sent,
                rim_recv_sem.at[stage, index, 1],
                to_below,
            )
            send(
                rim_send.at[index, stage, 1],
                rim_recv.at[index, stage, 0],
                sent,
                rim_recv_sem.at[stage, index, 0],
                to_above,
            )

    def finish(stage):
        for index in range(2):
            wait(rim_recv.at[index, stage, 0], rim_recv_sem.at[stage, index, 0])
            wait(rim_recv.at[index, stage, 1], rim_recv_sem.at[stage, index, 1])
            edge = block - HALO
            acc[index, stage, HALO : 2 * HALO, :] += rim_recv[index, stage, 0].astype(jnp.float32)
            acc[index, stage, HALO + edge : HALO + block, :] += rim_recv[index, stage, 1].astype(
                jnp.float32
            )
            results[2 + index, stage] = acc[index, stage, HALO : HALO + block, :].astype(
                jnp.bfloat16
            )

    def rows_of(array, stage, owner):
        return results.at[array, stage, pl.ds(pl.multiple_of(owner * tok, tok), tok), :]

    def issue_out(stage, arrays):
        for array in arrays:
            via = to_right if array % 2 == 0 else to_left
            send(
                rows_of(array, stage, far),
                relay_out.at[array, stage],
                out_send.at[array],
                back_recv.at[stage, array],
                via,
            )
        for array in arrays:
            arrived = out_recv.at[array]
            sent = out_send.at[array]
            mine = columns(outs[array], me, stage)
            send(rows_of(array, stage, right), mine, sent, arrived, to_right)
            send(rows_of(array, stage, left), mine, sent, arrived, to_left)
            pltpu.make_async_copy(rows_of(array, stage, me), mine, arrived).start()

    def pass_out(stage, arrays):
        for array in arrays:
            wait(relay_out.at[array, stage], back_recv.at[stage, array])
            onward, origin = (to_right, left) if array % 2 == 0 else (to_left, right)
            send(
                relay_out.at[array, stage],
                columns(outs[array], origin, stage),
                back_send.at[array],
                out_recv.at[array],
                onward,
            )

    barrier = pltpu.get_barrier_semaphore()
    for device in (to_right, to_left, to_above, to_below):
        pl.semaphore_signal(barrier, inc=1, device_id=device, device_id_type=MESH)
    pl.semaphore_wait(barrier, 4)

    issue_in(0)
    tiles = block // TILE
    fill_bias(bias, clip_table, windows, blk * tiles, n_blk * tiles)
    pass_in(0)
    issue_in(1)
    send_halo(0)
    pass_in(1)
    issue_in(2)

    def step(index, carry):
        def run(ahead, action):
            stage = index + ahead

            @pl.when((stage >= 0) & (stage < heads))
            def _():
                action(stage)

        run(1, send_halo)
        run(2, pass_in)
        run(3, issue_in)
        run(0, compute)
        run(-1, finish)
        run(-1, lambda stage: issue_out(stage, range(4)))
        run(-2, lambda stage: pass_out(stage, range(4)))
        return carry

    lax.fori_loop(0, heads + 2, step, 0)

    for array in range(4):
        wait(outs[array], out_recv.at[array])
        wait(sources[array].at[:, pl.ds(0, 3 * heads * HD)], in_send.at[array])
        wait(relay_in.at[array], pass_send.at[array])
        wait(results.at[array, :, pl.ds(0, 3 * tok), :], out_send.at[array])
        wait(relay_out.at[array], back_send.at[array])
    for index in range(2):
        wait(rim_send.at[index], halo_send.at[index])
        wait(rim_send.at[index], rim_send_sem.at[index])


def hand_over(*refs):
    inner, outer, held, (arrived, left) = refs[:4], refs[4:8], refs[8], refs[9:]
    tok = held.shape[1]
    pieces = [(array, row) for row in range(0, tok, PIECE) for array in range(4)]

    def take(array, row):
        rows = pl.ds(row, PIECE)
        return pltpu.make_async_copy(
            inner[array].at[rows], held.at[array, rows], arrived.at[array, row // PIECE]
        )

    def put(array, row):
        rows = pl.ds(row, PIECE)
        return pltpu.make_async_copy(
            held.at[array, rows], outer[array].at[rows], left.at[array, row // PIECE]
        )

    for piece in pieces:
        take(*piece).start()
    for piece in pieces:
        take(*piece).wait()
        put(*piece).start()
    for piece in pieces:
        put(*piece).wait()


def on_device(n_seq, n_blk, queries, key_states, value_states, grad_out, clip_table, windows):
    tok, width = queries.shape
    heads = width // HD // n_seq
    block = tok * n_seq
    extended = block + 2 * HALO
    low = jnp.bfloat16
    hbm = pl.BlockSpec(memory_space=pl.ANY)
    smem = pl.BlockSpec(memory_space=pltpu.SMEM)
    dma = pltpu.SemaphoreType.DMA
    inner = pl.pallas_call(
        functools.partial(kernel, "seq", "blk", n_seq, n_blk, heads),
        out_shape=[jax.ShapeDtypeStruct((tok, width), low)] * 4,
        in_specs=[hbm] * 4 + [smem] * 2,
        out_specs=[hbm] * 4,
        scratch_shapes=[
            pltpu.VMEM((2, heads, extended, HD), low),
            pltpu.VMEM((2, heads, block, HD), low),
            pltpu.VMEM((4, heads, tok, HD), low),
            pltpu.VMEM((4, heads, block, HD), low),
            pltpu.VMEM((4, heads, tok, HD), low),
            pltpu.VMEM((2, heads, extended, HD), jnp.float32),
            pltpu.VMEM((2, heads, 2, HALO, HD), low),
            pltpu.VMEM((2, heads, 2, HALO, HD), low),
            pltpu.VMEM((block // TILE, extended), jnp.float32),
            dma((heads, 4)),
            dma((4,)),
            dma((heads, 4)),
            dma((4,)),
            dma((heads, 2, 2)),
            dma((2,)),
            dma((heads, 2, 2)),
            dma((2,)),
            dma((4,)),
            dma((4,)),
            dma((heads, 4)),
            dma((4,)),
        ],
        compiler_params=pltpu.CompilerParams(
            collective_id=0, has_side_effects=True, vmem_limit_bytes=60 * 1024 * 1024
        ),
        name="attention_with_exchange",
    )(queries, key_states, value_states, grad_out, clip_table.T, windows.T)
    return pl.pallas_call(
        hand_over,
        out_shape=[jax.ShapeDtypeStruct((tok, width), low)] * 4,
        in_specs=[hbm] * 4,
        out_specs=[hbm] * 4,
        scratch_shapes=[
            pltpu.VMEM((4, tok, width), low),
            dma((4, tok // PIECE)),
            dma((4, tok // PIECE)),
        ],
        name="hand_over",
    )(*inner)


def solution(mesh):
    rows = P(("blk", "seq"), None)
    return jax.shard_map(
        functools.partial(on_device, mesh.shape["seq"], mesh.shape["blk"]),
        mesh=mesh,
        in_specs=(rows, rows, rows, rows, P(), P()),
        out_specs=(rows, rows, rows, rows),
        check_vma=False,
    )
```
